32 devices in a mesh: boson: 8 (over z, x), block: 4 (over y, core).
Axes of the slice: x: 2, y: 2, z: 4, core: 2. Of those that a mesh axis runs over, the one named last changes fastest.
Arguments:
- gamma_ph: bfloat16 [32, 1024, 1024], P('boson', 'block'), may hold values from -6 to 6
- full_ph: bfloat16 [32, 1024, 1024], P('boson', 'block'), may hold values from -0.1875 to 0.1875
- chi_ph: float32 [32, 1024], P('boson'), may hold values from 0.3 to 3
- pp_vertex: bfloat16 [32, 1024, 1024], P('boson', 'block'), may hold values from -0.1875 to 0.1875
- chi_pp: float32 [32, 1024], P('boson'), may hold values from 0.3 to 3
- relabel: int32 [32, 16, 8], replicated, may hold values from 0 to 31, as said below
Outputs:
- vertex_new: bfloat16 [32, 1024, 1024], P('boson', 'block')
The draws below stay inside these ranges and needn't reach their ends.
Inputs may be any that keep to these rules, and one draw needn't show every extreme that they name: `relabel`: for each row tile and column block the table is a permutation of the 32 points. The owner of the target point (target // 4) is the source's owner (q // 4) plus a shift modulo 8, and both this shift and the target's position among its owner's points (target % 4) depend only on the row tile, the column block and q % 4. Row tiles b * 4 to (b + 1) * 4 - 1 form row block b; within one row block, at most 17 of the 128 triples of position, row tile and column block share a shift, and some shift is shared by exactly 17; in every row block the shifts 1, 4 and 7 each occur.
All inputs are finite; a program needn't handle non-finite values.
Results may differ from the reference program's by a relative error of at most 0.0063.
Values may be sent and summed in bfloat16 or wider, within the bound.
A program may use at most 128 MiB of HBM per device.

```python
import math
import jax
import jax.numpy as jnp
from jax import lax

M = 1024
CB = 8
RS = 4
RB = 16
QD = 4
QB = 32
CAP = 17
N_BOSON = 8
N_BLOCK = 4


def draw_relabel(key, part):
    item_total = QD * RS * CB
    blocks = []
    values = jnp.arange(N_BOSON, dtype=jnp.int32)
    for row_block in range(N_BLOCK):
        block_key = jax.random.fold_in(key, 101 + row_block)
        key_offset, key_mix, key_slot = jax.random.split(block_key, 3)
        ranks = jax.random.permutation(key_offset, N_BOSON).astype(jnp.int32) + 3
        ranks = jnp.where(values == 1, 0, ranks)
        ranks = jnp.where(values == N_BOSON // 2, 1, ranks)
        ranks = jnp.where(values == N_BOSON - 1, 2, ranks)
        shuffled = jnp.argsort(ranks, stable=True).astype(jnp.int32)
        spread = shuffled[jnp.arange(item_total) // CAP]
        spread = spread[jax.random.permutation(key_mix, item_total)].reshape(QD, RS * CB)
        position = jax.vmap(lambda subkey: jax.random.permutation(subkey, QD))(jax.random.split(key_slot, RS * CB)).T
        source = jnp.arange(N_BOSON, dtype=jnp.int32)[:, None, None]
        target_point = (source + spread[None]) % N_BOSON * QD + position[None]
        blocks.append(target_point.reshape(N_BOSON * QD, RS, CB).astype(jnp.int32))
    return jnp.stack(blocks, axis=1).reshape(N_BOSON * QD, RS * N_BLOCK, CB)


def steps_of(key, shape, cuts, smallest, top_value):
    factor_of = 1.0
    for dim, parts in cuts:
        heights = jax.random.uniform(jax.random.fold_in(jax.random.fold_in(key, 6), dim), (parts,), jnp.float32, smallest / len(cuts), top_value / len(cuts))
        factor_of = factor_of * jnp.repeat(jnp.exp(heights), shape[dim] // parts).reshape((-1,) + (1,) * (len(shape) - 1 - dim))
    return factor_of


def scatter_about(key, extent, deviation, reach, cuts=(), kind=jnp.bfloat16):
    array = jax.random.normal(key, extent, jnp.float32) * deviation
    if len(cuts) > 0:
        array = steps_of(key, extent, cuts, -0.22, 0.18) * array
    return jnp.clip(array, min=-reach, max=reach).astype(kind)


def setup_inputs(seed: int = 0) -> dict:
    arg_keys = jax.random.split(jax.random.key(seed), 7)
    gamma_ph = scatter_about(arg_keys[0], (QB, M, M), 1.0, 6.0, ((0, 8), (1, 4)))
    full_ph = scatter_about(arg_keys[1], (QB, M, M), M ** -0.5, 0.1875, ((0, 8), (1, 4)))
    chi_ph = jnp.clip(jnp.exp(math.log(3.0) - 2.3025851 * jax.random.uniform(arg_keys[2], (QB, M), jnp.float32) ** steps_of(arg_keys[2], (QB, M), ((0, 8),), -0.2, 0.2)), 0.3, 3.0)
    pp_vertex = scatter_about(arg_keys[3], (QB, M, M), M ** -0.5, 0.1875, ((0, 8), (1, 4)))
    chi_pp = jnp.clip(jnp.exp(math.log(3.0) - 2.3025851 * jax.random.uniform(arg_keys[4], (QB, M), jnp.float32) ** steps_of(arg_keys[4], (QB, M), ((0, 8),), -0.2, 0.2)), 0.3, 3.0)
    relabel = draw_relabel(jax.random.fold_in(arg_keys[6], 71), 0)
    return {"gamma_ph": gamma_ph, "full_ph": full_ph, "chi_ph": chi_ph, "pp_vertex": pp_vertex, "chi_pp": chi_pp, "relabel": relabel}


def to_tiles(matrix):
    return matrix.reshape(QB, RB, M // RB, CB, M // CB).transpose(0, 1, 3, 2, 4)


def from_tiles(tile_stack):
    return tile_stack.transpose(0, 1, 3, 2, 4).reshape(QB, M, M)


def bubble_product(left_side, column_scale, right_side):
    def single(inputs):
        left_one, scale_one, right_one = inputs
        scaled = (left_one.astype(jnp.float32) * scale_one[None, :]).astype(jnp.bfloat16)
        return jnp.dot(scaled, right_one, preferred_element_type=jnp.float32)
    return lax.map(single, (left_side, column_scale, right_side))


def reference(gamma_ph, full_ph, chi_ph, pp_vertex, chi_pp, relabel):
    phi_ph = bubble_product(gamma_ph, chi_ph, full_ph)
    ph_tiles = to_tiles(phi_ph.astype(jnp.bfloat16))
    row_index = jnp.broadcast_to(jnp.arange(RB, dtype=jnp.int32)[None, :, None], relabel.shape)
    col_index = jnp.broadcast_to(jnp.arange(CB, dtype=jnp.int32)[None, None, :], relabel.shape)
    pp_tiles = jnp.zeros_like(ph_tiles).at[relabel, row_index, col_index].set(ph_tiles)
    relabelled = from_tiles(pp_tiles)
    phi_pp = bubble_product(relabelled, chi_pp, pp_vertex).astype(jnp.bfloat16)
    returned = to_tiles(phi_pp)[relabel, row_index, col_index]
    vertex_new = gamma_ph.astype(jnp.float32) + phi_ph + from_tiles(returned).astype(jnp.float32)
    return vertex_new.astype(jnp.bfloat16)
```

```python
import functools
import jax
import jax.numpy as jnp
from jax import lax
from jax.experimental import pallas as pl
from jax.experimental.pallas import tpu as pltpu
from jax.sharding import PartitionSpec as P

MESH = pl.DeviceIdType.MESH
DMA = pltpu.SemaphoreType.DMA


class Gather:
    def __init__(self, nblock, shard, whole, bounce, sems):
        self.nblock, self.shard, self.whole, self.bounce = nblock, shard, whole, bounce
        self.far_s, self.far_r, self.near_s, self.near_r, self.fwd_s, self.fwd_r, self.loc = sems
        self.points, self.rows = shard.shape[0], shard.shape[1]
        self.boson = lax.axis_index("boson")
        self.here = lax.axis_index("block")
        self.partner = self.here + 1 - 2 * (self.here % 2)

    def peers(self):
        out = [self.partner]
        for j in range(1, self.nblock // 2):
            out.append((self.here + 2 * j) % self.nblock)
        return out

    def place(self, q, owner):
        return self.whole.at[q, pl.ds(pl.multiple_of(owner * self.rows, self.rows), self.rows)]

    def far(self, q, j, owner):
        return pltpu.make_async_remote_copy(
            src_ref=self.shard.at[q], dst_ref=self.place(q, owner),
            send_sem=self.far_s.at[j - 1, q], recv_sem=self.far_r.at[j - 1, q],
            device_id=(self.boson, (self.here + 2 * j) % self.nblock), device_id_type=MESH)

    def near(self, q, owner):
        return pltpu.make_async_remote_copy(
            src_ref=self.shard.at[q], dst_ref=self.place(q, owner),
            send_sem=self.near_s.at[q], recv_sem=self.near_r.at[q],
            device_id=(self.boson, self.partner), device_id_type=MESH)

    def forward(self, q, j, owner):
        return pltpu.make_async_remote_copy(
            src_ref=self.place(q, owner), dst_ref=self.place(q, owner),
            send_sem=self.fwd_s.at[j - 1, q], recv_sem=self.fwd_r.at[j - 1, q],
            device_id=(self.boson, self.partner), device_id_type=MESH)

    def local_in(self):
        return pltpu.make_async_copy(self.shard, self.bounce, self.loc.at[0])

    def local_out(self):
        rows = pl.ds(pl.multiple_of(self.here * self.rows, self.rows), self.rows)
        return pltpu.make_async_copy(self.bounce, self.whole.at[:, rows], self.loc.at[1])

    def start(self):
        for q in range(self.points):
            for j in range(1, self.nblock // 2):
                self.far(q, j, self.here).start()
        for q in range(self.points):
            self.near(q, self.here).start()
        self.local_in().start()

    def relay(self):
        self.local_in().wait()
        self.local_out().start()
        for q in range(self.points):
            for j in range(1, self.nblock // 2):
                owner = (self.here + self.nblock - 2 * j) % self.nblock
                self.far(q, j, owner).wait_recv()
                self.forward(q, j, owner).start()

    def finish(self):
        self.local_out().wait()
        for q in range(self.points):
            self.near(q, self.here).wait_send()
            self.near(q, self.partner).wait_recv()
            for j in range(1, self.nblock // 2):
                owner = (self.here + self.nblock - 2 * j) % self.nblock
                twin = (self.partner + self.nblock - 2 * j) % self.nblock
                self.far(q, j, self.here).wait_send()
                self.forward(q, j, owner).wait_send()
                self.forward(q, j, twin).wait_recv()


def gather_scratch(nblock, shard):
    far = max(nblock // 2 - 1, 1)
    points = shard.shape[0]
    return [
        pltpu.VMEM(shard.shape, shard.dtype),
        DMA((far, points)), DMA((far, points)), DMA((points,)), DMA((points,)),
        DMA((far, points)), DMA((far, points)), DMA((2,)),
    ]


class Exchange:
    def __init__(self, nboson, outgoing, incoming, bounce, send, recv, loc):
        self.n, self.outgoing, self.incoming, self.bounce = nboson, outgoing, incoming, bounce
        self.send, self.recv, self.loc = send, recv, loc
        self.boson = lax.axis_index("boson")
        self.block = lax.axis_index("block")

    def peers(self):
        return [(self.boson + s) % self.n for s in range(1, self.n)]

    def copy(self, s, slot):
        dest = (self.boson + s) % self.n
        return pltpu.make_async_remote_copy(
            src_ref=self.outgoing.at[dest], dst_ref=self.incoming.at[slot],
            send_sem=self.send.at[s], recv_sem=self.recv.at[s],
            device_id=(dest, self.block), device_id_type=MESH)

    def local_in(self):
        return pltpu.make_async_copy(self.outgoing.at[self.boson], self.bounce, self.loc.at[0])

    def local_out(self):
        return pltpu.make_async_copy(self.bounce, self.incoming.at[self.boson], self.loc.at[1])

    def order(self):
        mid = self.n // 2
        return sorted(range(1, self.n), key=lambda s: (abs(s - mid), s))

    def start(self):
        for s in self.order():
            self.copy(s, self.boson).start()
        self.local_in().start()

    def finish(self):
        self.local_in().wait()
        self.local_out().start()
        for s in self.order():
            self.copy(s, self.boson).wait_send()
            self.copy(s, (self.boson + self.n - s) % self.n).wait_recv()
        self.local_out().wait()


def exchange_scratch(nboson, outgoing):
    return [
        pltpu.VMEM(outgoing.shape[1:], outgoing.dtype),
        DMA((nboson,)), DMA((nboson,)), DMA((2,)),
    ]


def greet(block_peers, boson_peers):
    barrier = pltpu.get_barrier_semaphore()
    boson, block = lax.axis_index("boson"), lax.axis_index("block")
    for peer in block_peers:
        pl.semaphore_signal(barrier, inc=1, device_id=(boson, peer), device_id_type=MESH)
    for peer in boson_peers:
        pl.semaphore_signal(barrier, inc=1, device_id=(peer, block), device_id_type=MESH)
    pl.semaphore_wait(barrier, len(block_peers) + len(boson_peers))


def gather_kernel(nblock, shard, whole, bounce, *sems):
    gather = Gather(nblock, shard, whole, bounce, sems)
    greet(gather.peers(), [])
    gather.start()
    gather.relay()
    gather.finish()


def both_kernel(nblock, nboson, shard, outgoing, whole, incoming, *scratch):
    gather = Gather(nblock, shard, whole, scratch[0], scratch[1:8])
    exchange = Exchange(nboson, outgoing, incoming, *scratch[8:])
    greet(gather.peers(), exchange.peers())
    exchange.start()
    gather.start()
    gather.relay()
    gather.finish()
    exchange.finish()


def exchange_kernel(nboson, outgoing, incoming, *scratch):
    exchange = Exchange(nboson, outgoing, incoming, *scratch)
    greet([], exchange.peers())
    exchange.start()
    exchange.finish()


ANY = pl.BlockSpec(memory_space=pl.ANY)


def remote_call(body, operands, outs, scratch, ident, name):
    return pl.pallas_call(
        body, out_shape=outs, in_specs=[ANY] * len(operands),
        out_specs=jax.tree.map(lambda _: ANY, outs), scratch_shapes=scratch, name=name,
        compiler_params=pltpu.CompilerParams(collective_id=ident, has_side_effects=True),
    )(*operands)


def row_of(chi, index):
    rows = lax.broadcasted_iota(jnp.int32, chi.shape, 0)
    return jnp.sum(jnp.where(rows == index, chi[...], 0.0), axis=0, keepdims=True)


def first_kernel(row_tiles, col_blocks, slots, gamma, chi, full, packed, base, scaled):
    q = pl.program_id(0)
    rows, order = gamma.shape[1], gamma.shape[2]
    high, wide = rows // row_tiles, order // col_blocks
    scaled[...] = (gamma[0].astype(jnp.float32) * row_of(chi, q)).astype(jnp.bfloat16)
    step = 2 * wide
    for start in range(0, order, step):
        phi = jnp.dot(scaled[...], full[0, :, start:start + step],
                      preferred_element_type=jnp.float32)
        base[0, :, start:start + step] = gamma[0, :, start:start + step].astype(jnp.float32) + phi
        wire = phi.astype(jnp.bfloat16)
        for r in range(row_tiles):
            for k in range(2):
                item = (q * row_tiles + r) * col_blocks + start // wide + k
                packed[slots[item]] = wire[r * high:(r + 1) * high, k * wide:(k + 1) * wide]


def second_kernel(row_tiles, col_blocks, slots, arrived, chi, full, packed, scaled):
    p = pl.program_id(0)
    rows, order = scaled.shape
    high, wide = rows // row_tiles, order // col_blocks
    chi_row = row_of(chi, p)
    for c in range(col_blocks):
        chi_c = chi_row[:, c * wide:(c + 1) * wide]
        for r in range(row_tiles):
            tile = arrived[slots[(p * row_tiles + r) * col_blocks + c]]
            scaled[r * high:(r + 1) * high, c * wide:(c + 1) * wide] = (
                tile.astype(jnp.float32) * chi_c).astype(jnp.bfloat16)
    step = 2 * wide
    for start in range(0, order, step):
        wire = jnp.dot(scaled[...], full[0, :, start:start + step],
                       preferred_element_type=jnp.float32).astype(jnp.bfloat16)
        for r in range(row_tiles):
            for k in range(2):
                item = (p * row_tiles + r) * col_blocks + start // wide + k
                packed[slots[item]] = wire[r * high:(r + 1) * high, k * wide:(k + 1) * wide]


def last_kernel(row_tiles, col_blocks, slots, arrived, base, out):
    q = pl.program_id(0)
    rows, order = out.shape[1], out.shape[2]
    high, wide = rows // row_tiles, order // col_blocks
    for r in range(row_tiles):
        for c in range(col_blocks):
            tile = arrived[slots[(q * row_tiles + r) * col_blocks + c]]
            place = (0, slice(r * high, (r + 1) * high), slice(c * wide, (c + 1) * wide))
            out[place] = (base[place] + tile.astype(jnp.float32)).astype(jnp.bfloat16)


def point_spec(shape):
    return pl.BlockSpec((1,) + tuple(shape[1:]), lambda i, *_: (i, 0, 0))


def whole_spec(shape):
    return pl.BlockSpec(tuple(shape), lambda i, *_: (0,) * len(shape))


def tables(relabel, points, row_tiles, nboson, capacity):
    boson, block = lax.axis_index("boson"), lax.axis_index("block")
    col_blocks = relabel.shape[2]
    per_point = row_tiles * col_blocks
    total = points * per_point
    own = lax.dynamic_slice(
        relabel, (boson * points, block * row_tiles, 0), (points, row_tiles, col_blocks)
    ).reshape(total)
    shifts = (own // points - boson) % nboson
    items = jnp.arange(total, dtype=jnp.int32)
    target = own % points * per_point + items % per_point
    earlier = (shifts[None, :] == shifts[:, None]) & (items[None, :] < items[:, None])
    rank = jnp.sum(earlier.astype(jnp.int32), axis=1)
    send_slot = (boson + shifts) % nboson * capacity + rank
    recv_slot = (boson - shifts) % nboson * capacity + rank
    hit = (target[None, :] == items[:, None]).astype(jnp.int32)
    back_slot = jnp.sum(hit * recv_slot[None, :], axis=1)
    return send_slot, back_slot


def local(nboson, nblock, gamma_ph, full_ph, chi_ph, pp_vertex, chi_pp, relabel):
    points, rows, order = gamma_ph.shape
    row_tiles, col_blocks = relabel.shape[1] // nblock, relabel.shape[2]
    high, wide = rows // row_tiles, order // col_blocks
    capacity = -(-(points * row_tiles * col_blocks) // nboson) + 1
    send_slot, back_slot = tables(relabel, points, row_tiles, nboson, capacity)
    shape = jax.ShapeDtypeStruct
    bf16, f32 = jnp.bfloat16, jnp.float32
    whole = shape((points, order, order), bf16)
    packed = shape((nboson * capacity, high, wide), bf16)
    slabs = shape((nboson, capacity, high, wide), bf16)
    scaled = pltpu.VMEM((rows, order), bf16)

    full = remote_call(
        functools.partial(gather_kernel, nblock), (full_ph,), whole,
        gather_scratch(nblock, full_ph), 0, "gather_full")
    outgoing, base = pl.pallas_call(
        functools.partial(first_kernel, row_tiles, col_blocks),
        out_shape=(packed, shape(gamma_ph.shape, f32)), name="first",
        grid_spec=pltpu.PrefetchScalarGridSpec(
            num_scalar_prefetch=1, grid=(points,),
            in_specs=[point_spec(gamma_ph.shape), whole_spec(chi_ph.shape), point_spec(whole.shape)],
            out_specs=(whole_spec(packed.shape), point_spec(gamma_ph.shape)),
            scratch_shapes=[scaled]),
    )(send_slot, gamma_ph, chi_ph, full)
    pp_full, incoming = remote_call(
        functools.partial(both_kernel, nblock, nboson),
        (pp_vertex, outgoing.reshape(slabs.shape)), (whole, slabs),
        gather_scratch(nblock, pp_vertex) + exchange_scratch(nboson, slabs), 1, "both")
    outgoing_back = pl.pallas_call(
        functools.partial(second_kernel, row_tiles, col_blocks),
        out_shape=packed, name="second",
        grid_spec=pltpu.PrefetchScalarGridSpec(
            num_scalar_prefetch=1, grid=(points,),
            in_specs=[whole_spec(packed.shape), whole_spec(chi_pp.shape), point_spec(whole.shape)],
            out_specs=whole_spec(packed.shape), scratch_shapes=[scaled]),
    )(back_slot, incoming.reshape(packed.shape), chi_pp, pp_full)
    incoming_back = remote_call(
        functools.partial(exchange_kernel, nboson), (outgoing_back.reshape(slabs.shape),), slabs,
        exchange_scratch(nboson, slabs), 2, "back")
    return pl.pallas_call(
        functools.partial(last_kernel, row_tiles, col_blocks),
        out_shape=shape(gamma_ph.shape, bf16), name="last",
        grid_spec=pltpu.PrefetchScalarGridSpec(
            num_scalar_prefetch=1, grid=(points,),
            in_specs=[whole_spec(packed.shape), point_spec(gamma_ph.shape)],
            out_specs=point_spec(gamma_ph.shape)),
    )(send_slot, incoming_back.reshape(packed.shape), base)


def solution(mesh):
    placed = (
        P("boson", "block", None),
        P("boson", "block", None),
        P("boson", None),
        P("boson", "block", None),
        P("boson", None),
        P(),
    )
    return jax.shard_map(
        functools.partial(local, mesh.shape["boson"], mesh.shape["block"]), mesh=mesh,
        in_specs=placed, out_specs=P("boson", "block", None), check_vma=False,
    )
```

```python
import functools
import jax
import jax.numpy as jnp
from jax import lax
from jax.experimental import pallas as pl
from jax.experimental.pallas import tpu as pltpu
from jax.sharding import PartitionSpec as P

MESH = pl.DeviceIdType.MESH
DMA = pltpu.SemaphoreType.DMA
PARTS = 2


def loop(start, stop, body):
    lax.fori_loop(start, stop, lambda i, carry: (body(i), carry)[1], 0)


class Gather:
    def __init__(self, nblock, shard, whole, sems):
        self.nblock, self.shard, self.whole = nblock, shard, whole
        self.far_s, self.far_r, self.near_s, self.near_r, self.fwd_s, self.fwd_r, self.loc = sems
        self.points, self.rows, order = shard.shape
        self.cols = order // PARTS
        self.chunks = self.points * PARTS
        self.boson = lax.axis_index("boson")
        self.here = lax.axis_index("block")
        self.partner = self.here + 1 - 2 * (self.here % 2)

    def peers(self):
        out = [self.partner]
        for j in range(1, self.nblock // 2):
            out.append((self.here + 2 * j) % self.nblock)
        return out

    def columns(self, g):
        return pl.ds(pl.multiple_of(g % PARTS * self.cols, self.cols), self.cols)

    def source(self, g):
        return self.shard.at[g // PARTS, :, self.columns(g)]

    def place(self, g, owner):
        rows = pl.ds(pl.multiple_of(owner * self.rows, self.rows), self.rows)
        return self.whole.at[g // PARTS, rows, self.columns(g)]

    def far(self, g, j, owner):
        return pltpu.make_async_remote_copy(
            src_ref=self.source(g), dst_ref=self.place(g, owner),
            send_sem=self.far_s.at[j - 1, g], recv_sem=self.far_r.at[j - 1, g],
            device_id=(self.boson, (self.here + 2 * j) % self.nblock), device_id_type=MESH)

    def near(self, g, owner):
        return pltpu.make_async_remote_copy(
            src_ref=self.source(g), dst_ref=self.place(g, owner),
            send_sem=self.near_s.at[g], recv_sem=self.near_r.at[g],
            device_id=(self.boson, self.partner), device_id_type=MESH)

    def forward(self, g, j, owner):
        return pltpu.make_async_remote_copy(
            src_ref=self.place(g, owner), dst_ref=self.place(g, owner),
            send_sem=self.fwd_s.at[j - 1, g], recv_sem=self.fwd_r.at[j - 1, g],
            device_id=(self.boson, self.partner), device_id_type=MESH)

    def own(self):
        rows = pl.ds(pl.multiple_of(self.here * self.rows, self.rows), self.rows)
        return pltpu.make_async_copy(self.shard, self.whole.at[:, rows], self.loc)

    def each_far(self, act):
        for j in range(1, self.nblock // 2):
            act(j)

    def start(self):
        def one(g):
            self.each_far(lambda j: self.far(g, j, self.here).start())
            self.near(g, self.here).start()
        loop(0, self.chunks, one)

    def relay(self, g):
        def one(j):
            owner = (self.here + self.nblock - 2 * j) % self.nblock
            self.far(g, j, owner).wait_recv()
            self.forward(g, j, owner).start()
        self.each_far(one)

    def arrived(self, g):
        self.near(g, self.partner).wait_recv()
        def one(j):
            twin = (self.partner + self.nblock - 2 * j) % self.nblock
            self.forward(g, j, twin).wait_recv()
        self.each_far(one)

    def sent_far(self):
        loop(0, self.chunks,
             lambda g: self.each_far(lambda j: self.far(g, j, self.here).wait_send()))

    def sent_near(self):
        def one(g):
            self.near(g, self.here).wait_send()
            def fwd(j):
                owner = (self.here + self.nblock - 2 * j) % self.nblock
                self.forward(g, j, owner).wait_send()
            self.each_far(fwd)
        loop(0, self.chunks, one)


def gather_scratch(nblock, points):
    far, chunks = max(nblock // 2 - 1, 1), points * PARTS
    return [DMA((far, chunks)), DMA((far, chunks)), DMA((chunks,)), DMA((chunks,)),
            DMA((far, chunks)), DMA((far, chunks)), DMA]


class Exchange:
    def __init__(self, nboson, outgoing, incoming, send, recv):
        self.n, self.outgoing, self.incoming = nboson, outgoing, incoming
        self.send, self.recv = send, recv
        self.boson = lax.axis_index("boson")
        self.block = lax.axis_index("block")

    def peers(self):
        return [(self.boson + s) % self.n for s in range(1, self.n)]

    def shift(self, i):
        return self.n // 2 + (1 - 2 * (i % 2)) * ((i + 1) // 2)

    def copy(self, s, slot):
        dest = (self.boson + s) % self.n
        return pltpu.make_async_remote_copy(
            src_ref=self.outgoing.at[dest], dst_ref=self.incoming.at[slot],
            send_sem=self.send.at[s], recv_sem=self.recv.at[s],
            device_id=(dest, self.block), device_id_type=MESH)

    def pack(self, target, dest, tiles, table):
        capacity = target.shape[1]
        for k in range(capacity):
            target[dest, k] = tiles[table[dest * capacity + k]]

    def pack_and_start(self, tiles, table):
        def pack(i):
            self.pack(self.outgoing, (self.boson + self.shift(i)) % self.n, tiles, table)
        pack(0)
        def one(i):
            pack(i)
            self.copy(self.shift(i - 1), self.boson).start()
        loop(1, self.n - 1, one)
        self.pack(self.incoming, self.boson, tiles, table)
        self.copy(self.shift(self.n - 2), self.boson).start()

    def received(self):
        loop(1, self.n, lambda s: self.copy(s, (self.boson + self.n - s) % self.n).wait_recv())

    def sent(self):
        loop(1, self.n, lambda s: self.copy(s, self.boson).wait_send())


def greet(block_peers, boson_peers):
    barrier = pltpu.get_barrier_semaphore()
    boson, block = lax.axis_index("boson"), lax.axis_index("block")
    for peer in block_peers:
        pl.semaphore_signal(barrier, inc=1, device_id=(boson, peer), device_id_type=MESH)
    for peer in boson_peers:
        pl.semaphore_signal(barrier, inc=1, device_id=(peer, block), device_id_type=MESH)
    pl.semaphore_wait(barrier, len(block_peers) + len(boson_peers))


def kernel(nboson, nblock, row_tiles, col_blocks,
           send_slot, item_of, back_slot, back_item_of,
           gamma_in, full_in, chi_ph, pp_in, chi_pp, out,
           full, pp, gamma, scaled, base, tiles, packed, landed, back, returned, result,
           gamma_sem, out_sem, ahead_s, ahead_r, home_s, home_r, *gather_sems):
    half = len(gather_sems) // 2
    first = Gather(nblock, full_in, full, gather_sems[:half])
    second = Gather(nblock, pp_in, pp, gather_sems[half:])
    ahead = Exchange(nboson, packed, landed, ahead_s, ahead_r)
    home = Exchange(nboson, back, returned, home_s, home_r)
    points, rows, order = gamma.shape
    high, wide = rows // row_tiles, order // col_blocks
    step = 2 * wide
    load_gamma = pltpu.make_async_copy(gamma_in, gamma, gamma_sem)

    first.own().start()
    load_gamma.start()
    second.own().start()
    greet(first.peers(), ahead.peers())
    first.start()

    load_gamma.wait()
    for q in range(points):
        scaled[q] = (gamma[q].astype(jnp.float32) * chi_ph[q:q + 1, :]).astype(jnp.bfloat16)
    first.own().wait()

    def cut(wire, q, column):
        for r in range(row_tiles):
            for k in range(2):
                item = (q * row_tiles + r) * col_blocks + column * 2 + k
                tiles[item] = wire[r * high:(r + 1) * high, k * wide:(k + 1) * wide]

    def product(whole, q, column):
        at = pl.ds(pl.multiple_of(column * step, step), step)
        return at, jnp.dot(scaled[q], whole[q, :, at], preferred_element_type=jnp.float32)

    per_part = order // step // PARTS

    def compute(g):
        first.arrived(g)
        q = g // PARTS
        for n in range(per_part):
            column = g % PARTS * per_part + n
            at, phi = product(full, q, column)
            base[q, :, at] = gamma[q, :, at].astype(jnp.float32) + phi
            cut(phi.astype(jnp.bfloat16), q, column)

    first.relay(0)
    def one(g):
        first.relay(g)
        compute(g - 1)
    loop(1, first.chunks, one)
    first.sent_far()
    second.start()
    compute(first.chunks - 1)
    ahead.pack_and_start(tiles, item_of)

    loop(0, second.chunks, second.relay)
    first.sent_near()
    second.own().wait()
    loop(0, second.chunks, second.arrived)
    ahead.received()

    capacity = landed.shape[1]
    flat = landed.reshape(nboson * capacity, high, wide)
    for p in range(points):
        for c in range(col_blocks):
            chi = chi_pp[p:p + 1, c * wide:(c + 1) * wide]
            for r in range(row_tiles):
                tile = flat[back_slot[(p * row_tiles + r) * col_blocks + c]]
                scaled[p, r * high:(r + 1) * high, c * wide:(c + 1) * wide] = (
                    tile.astype(jnp.float32) * chi).astype(jnp.bfloat16)
    def point(p):
        for column in range(order // step):
            _, phi = product(pp, p, column)
            cut(phi.astype(jnp.bfloat16), p, column)
    loop(0, points, point)
    home.pack_and_start(tiles, back_item_of)
    ahead.sent()
    second.sent_far()
    second.sent_near()
    home.received()

    flat_back = returned.reshape(nboson * capacity, high, wide)
    def finish(q):
        for r in range(row_tiles):
            for c in range(col_blocks):
                tile = flat_back[send_slot[(q * row_tiles + r) * col_blocks + c]]
                at = (q, slice(r * high, (r + 1) * high), slice(c * wide, (c + 1) * wide))
                result[at] = (base[at] + tile.astype(jnp.float32)).astype(jnp.bfloat16)
        pltpu.make_async_copy(result.at[q], out.at[q], out_sem.at[q]).start()
    loop(0, points, finish)
    home.sent()
    loop(0, points,
         lambda q: pltpu.make_async_copy(result.at[q], out.at[q], out_sem.at[q]).wait())


def tables(relabel, points, row_tiles, nboson, capacity):
    boson, block = lax.axis_index("boson"), lax.axis_index("block")
    col_blocks = relabel.shape[2]
    per_point = row_tiles * col_blocks
    total = points * per_point
    own = lax.dynamic_slice(
        relabel, (boson * points, block * row_tiles, 0), (points, row_tiles, col_blocks)
    ).reshape(total)
    shifts = (own // points - boson) % nboson
    items = jnp.arange(total, dtype=jnp.int32)
    slots = jnp.arange(nboson * capacity, dtype=jnp.int32)
    target = own % points * per_point + items % per_point
    earlier = (shifts[None, :] == shifts[:, None]) & (items[None, :] < items[:, None])
    rank = jnp.sum(earlier.astype(jnp.int32), axis=1)
    send_slot = (boson + shifts) % nboson * capacity + rank
    recv_slot = (boson - shifts) % nboson * capacity + rank

    def pick(keys, wanted, values):
        hit = (keys[None, :] == wanted[:, None]).astype(jnp.int32)
        return jnp.sum(hit * values[None, :], axis=1)

    return (send_slot, pick(send_slot, slots, items), pick(target, items, recv_slot),
            pick(recv_slot, slots, target))


def local(nboson, nblock, gamma_ph, full_ph, chi_ph, pp_vertex, chi_pp, relabel):
    points, rows, order = gamma_ph.shape
    row_tiles, col_blocks = relabel.shape[1] // nblock, relabel.shape[2]
    high, wide = rows // row_tiles, order // col_blocks
    total = points * row_tiles * col_blocks
    capacity = -(-total // nboson) + 1
    bf16, f32 = jnp.bfloat16, jnp.float32
    whole = pltpu.VMEM((points, order, order), bf16)
    shard = pltpu.VMEM(gamma_ph.shape, bf16)
    slabs = pltpu.VMEM((nboson, capacity, high, wide), bf16)
    smem = pl.BlockSpec(memory_space=pltpu.SMEM)
    vmem = pl.BlockSpec(memory_space=pltpu.VMEM)
    hbm = pl.BlockSpec(memory_space=pl.ANY)
    return pl.pallas_call(
        functools.partial(kernel, nboson, nblock, row_tiles, col_blocks),
        out_shape=jax.ShapeDtypeStruct(gamma_ph.shape, bf16), name="window",
        in_specs=[smem] * 4 + [hbm, hbm, vmem, hbm, vmem], out_specs=hbm,
        scratch_shapes=[
            whole, whole, shard, shard, pltpu.VMEM(gamma_ph.shape, f32),
            pltpu.VMEM((total, high, wide), bf16), slabs, slabs, slabs, slabs, shard,
            DMA, DMA((points,)), DMA((nboson,)), DMA((nboson,)), DMA((nboson,)), DMA((nboson,)),
        ] + gather_scratch(nblock, points) + gather_scratch(nblock, points),
        compiler_params=pltpu.CompilerParams(
            collective_id=0, has_side_effects=True, vmem_limit_bytes=60 * 1024 * 1024),
    )(*tables(relabel, points, row_tiles, nboson, capacity),
      gamma_ph, full_ph, chi_ph, pp_vertex, chi_pp)


def solution(mesh):
    placed = (
        P("boson", "block", None),
        P("boson", "block", None),
        P("boson", None),
        P("boson", "block", None),
        P("boson", None),
        P(),
    )
    return jax.shard_map(
        functools.partial(local, mesh.shape["boson"], mesh.shape["block"]), mesh=mesh,
        in_specs=placed, out_specs=P("boson", "block", None), check_vma=False,
    )
```

```python
import functools
import jax
import jax.numpy as jnp
from jax import lax
from jax.experimental import pallas as pl
from jax.experimental.pallas import tpu as pltpu
from jax.sharding import PartitionSpec as P

MESH = pl.DeviceIdType.MESH
DMA = pltpu.SemaphoreType.DMA
PARTS = 4


def loop(start, stop, body):
    lax.fori_loop(start, stop, lambda i, carry: (body(i), carry)[1], 0)


class Gather:
    def __init__(self, nblock, shard, whole, sems):
        self.nblock, self.shard, self.whole = nblock, shard, whole
        self.far_s, self.far_r, self.near_s, self.near_r, self.fwd_s, self.fwd_r, self.loc = sems
        self.points, self.rows, order = shard.shape
        self.cols = order // PARTS
        self.chunks = self.points * PARTS
        self.boson = lax.axis_index("boson")
        self.here = lax.axis_index("block")
        self.partner = self.here + 1 - 2 * (self.here % 2)

    def peers(self):
        out = [self.partner]
        for j in range(1, self.nblock // 2):
            out.append((self.here + 2 * j) % self.nblock)
        return out

    def columns(self, g):
        return pl.ds(pl.multiple_of(g % PARTS * self.cols, self.cols), self.cols)

    def source(self, g):
        return self.shard.at[g // PARTS, :, self.columns(g)]

    def place(self, g, owner):
        rows = pl.ds(pl.multiple_of(owner * self.rows, self.rows), self.rows)
        return self.whole.at[g // PARTS, rows, self.columns(g)]

    def far(self, g, j, owner):
        return pltpu.make_async_remote_copy(
            src_ref=self.source(g), dst_ref=self.place(g, owner),
            send_sem=self.far_s.at[j - 1, g], recv_sem=self.far_r.at[j - 1, g],
            device_id=(self.boson, (self.here + 2 * j) % self.nblock), device_id_type=MESH)

    def near(self, g, owner):
        return pltpu.make_async_remote_copy(
            src_ref=self.source(g), dst_ref=self.place(g, owner),
            send_sem=self.near_s.at[g], recv_sem=self.near_r.at[g],
            device_id=(self.boson, self.partner), device_id_type=MESH)

    def forward(self, g, j, owner):
        return pltpu.make_async_remote_copy(
            src_ref=self.place(g, owner), dst_ref=self.place(g, owner),
            send_sem=self.fwd_s.at[j - 1, g], recv_sem=self.fwd_r.at[j - 1, g],
            device_id=(self.boson, self.partner), device_id_type=MESH)

    def own(self):
        rows = pl.ds(pl.multiple_of(self.here * self.rows, self.rows), self.rows)
        return pltpu.make_async_copy(self.shard, self.whole.at[:, rows], self.loc)

    def each_far(self, act):
        for j in range(1, self.nblock // 2):
            act(j)

    def start(self):
        def one(g):
            self.each_far(lambda j: self.far(g, j, self.here).start())
            self.near(g, self.here).start()
        loop(0, self.chunks, one)

    def relay(self, g):
        def one(j):
            owner = (self.here + self.nblock - 2 * j) % self.nblock
            self.far(g, j, owner).wait_recv()
            self.forward(g, j, owner).start()
        self.each_far(one)

    def arrived(self, g):
        self.near(g, self.partner).wait_recv()
        def one(j):
            twin = (self.partner + self.nblock - 2 * j) % self.nblock
            self.forward(g, j, twin).wait_recv()
        self.each_far(one)

    def sent_far(self):
        loop(0, self.chunks,
             lambda g: self.each_far(lambda j: self.far(g, j, self.here).wait_send()))

    def sent_near(self):
        def one(g):
            self.near(g, self.here).wait_send()
            def fwd(j):
                owner = (self.here + self.nblock - 2 * j) % self.nblock
                self.forward(g, j, owner).wait_send()
            self.each_far(fwd)
        loop(0, self.chunks, one)


def gather_scratch(nblock, points):
    far, chunks = max(nblock // 2 - 1, 1), points * PARTS
    return [DMA((far, chunks)), DMA((far, chunks)), DMA((chunks,)), DMA((chunks,)),
            DMA((far, chunks)), DMA((far, chunks)), DMA]


class Exchange:
    def __init__(self, nboson, outgoing, incoming, send, recv):
        self.n, self.outgoing, self.incoming = nboson, outgoing, incoming
        self.send, self.recv = send, recv
        self.boson = lax.axis_index("boson")
        self.block = lax.axis_index("block")

    def peers(self):
        return [(self.boson + s) % self.n for s in range(1, self.n)]

    def shift(self, i):
        return self.n // 2 + (1 - 2 * (i % 2)) * ((i + 1) // 2)

    def copy(self, s, slot):
        dest = (self.boson + s) % self.n
        return pltpu.make_async_remote_copy(
            src_ref=self.outgoing.at[dest], dst_ref=self.incoming.at[slot],
            send_sem=self.send.at[s], recv_sem=self.recv.at[s],
            device_id=(dest, self.block), device_id_type=MESH)

    def pack(self, target, dest, tiles, table):
        capacity = target.shape[1]
        for k in range(capacity):
            target[dest, k] = tiles[table[dest * capacity + k]]

    def pack_and_start(self, tiles, table):
        def pack(i):
            self.pack(self.outgoing, (self.boson + self.shift(i)) % self.n, tiles, table)
        pack(0)
        def one(i):
            pack(i)
            self.copy(self.shift(i - 1), self.boson).start()
        loop(1, self.n - 1, one)
        self.pack(self.incoming, self.boson, tiles, table)
        self.copy(self.shift(self.n - 2), self.boson).start()

    def received(self):
        loop(1, self.n, lambda s: self.copy(s, (self.boson + self.n - s) % self.n).wait_recv())

    def sent(self):
        loop(1, self.n, lambda s: self.copy(s, self.boson).wait_send())


def greet(block_peers, boson_peers):
    barrier = pltpu.get_barrier_semaphore()
    boson, block = lax.axis_index("boson"), lax.axis_index("block")
    for peer in block_peers:
        pl.semaphore_signal(barrier, inc=1, device_id=(boson, peer), device_id_type=MESH)
    for peer in boson_peers:
        pl.semaphore_signal(barrier, inc=1, device_id=(peer, block), device_id_type=MESH)
    pl.semaphore_wait(barrier, len(block_peers) + len(boson_peers))


def kernel(nboson, nblock, row_tiles, col_blocks,
           send_slot, item_of, back_slot, back_item_of,
           gamma_in, full_in, chi_ph, pp_in, chi_pp, out,
           full, pp, gamma, scaled, base, tiles, packed, landed, back, returned,
           gamma_sem, ahead_s, ahead_r, home_s, home_r, *gather_sems):
    half = len(gather_sems) // 2
    first = Gather(nblock, full_in, full, gather_sems[:half])
    second = Gather(nblock, pp_in, pp, gather_sems[half:])
    ahead = Exchange(nboson, packed, landed, ahead_s, ahead_r)
    home = Exchange(nboson, back, returned, home_s, home_r)
    points, rows, order = gamma.shape
    high, wide = rows // row_tiles, order // col_blocks
    step = 2 * wide
    load_gamma = pltpu.make_async_copy(gamma_in, gamma, gamma_sem)

    first.own().start()
    load_gamma.start()
    second.own().start()
    greet(first.peers(), ahead.peers())
    first.start()

    load_gamma.wait()
    for q in range(points):
        scaled[q] = (gamma[q].astype(jnp.float32) * chi_ph[q:q + 1, :]).astype(jnp.bfloat16)
    first.own().wait()

    def cut(wire, q, column):
        for r in range(row_tiles):
            for k in range(2):
                item = (q * row_tiles + r) * col_blocks + column * 2 + k
                tiles[item] = wire[r * high:(r + 1) * high, k * wide:(k + 1) * wide]

    def product(whole, q, column):
        at = pl.ds(pl.multiple_of(column * step, step), step)
        return at, jnp.dot(scaled[q], whole[q, :, at], preferred_element_type=jnp.float32)

    per_part = order // step // PARTS

    def compute(g):
        first.arrived(g)
        q = g // PARTS
        for n in range(per_part):
            column = g % PARTS * per_part + n
            at, phi = product(full, q, column)
            base[q, :, at] = gamma[q, :, at].astype(jnp.float32) + phi
            cut(phi.astype(jnp.bfloat16), q, column)

    first.relay(0)
    def one(g):
        first.relay(g)
        compute(g - 1)
    loop(1, first.chunks, one)
    first.sent_far()
    second.start()
    compute(first.chunks - 1)
    ahead.pack_and_start(tiles, item_of)

    loop(0, second.chunks, second.relay)
    first.sent_near()
    second.own().wait()
    loop(0, second.chunks, second.arrived)
    ahead.received()

    capacity = landed.shape[1]
    flat = landed.reshape(nboson * capacity, high, wide)
    for p in range(points):
        for c in range(col_blocks):
            chi = chi_pp[p:p + 1, c * wide:(c + 1) * wide]
            for r in range(row_tiles):
                tile = flat[back_slot[(p * row_tiles + r) * col_blocks + c]]
                scaled[p, r * high:(r + 1) * high, c * wide:(c + 1) * wide] = (
                    tile.astype(jnp.float32) * chi).astype(jnp.bfloat16)
    def point(p):
        for column in range(order // step):
            _, phi = product(pp, p, column)
            cut(phi.astype(jnp.bfloat16), p, column)
    loop(0, points, point)
    home.pack_and_start(tiles, back_item_of)
    ahead.sent()
    second.sent_far()
    second.sent_near()
    home.received()

    flat_back = returned.reshape(nboson * capacity, high, wide)
    def finish(q):
        for r in range(row_tiles):
            for c in range(col_blocks):
                tile = flat_back[send_slot[(q * row_tiles + r) * col_blocks + c]]
                at = (q, slice(r * high, (r + 1) * high), slice(c * wide, (c + 1) * wide))
                out[at] = (base[at] + tile.astype(jnp.float32)).astype(jnp.bfloat16)
    loop(0, points, finish)
    home.sent()


def tables(relabel, points, row_tiles, nboson, capacity):
    boson, block = lax.axis_index("boson"), lax.axis_index("block")
    col_blocks = relabel.shape[2]
    per_point = row_tiles * col_blocks
    total = points * per_point
    own = lax.dynamic_slice(
        relabel, (boson * points, block * row_tiles, 0), (points, row_tiles, col_blocks)
    ).reshape(total)
    shifts = (own // points - boson) % nboson
    items = jnp.arange(total, dtype=jnp.int32)
    slots = jnp.arange(nboson * capacity, dtype=jnp.int32)
    target = own % points * per_point + items % per_point
    earlier = (shifts[None, :] == shifts[:, None]) & (items[None, :] < items[:, None])
    rank = jnp.sum(earlier.astype(jnp.int32), axis=1)
    send_slot = (boson + shifts) % nboson * capacity + rank
    recv_slot = (boson - shifts) % nboson * capacity + rank

    def pick(keys, wanted, values):
        hit = (keys[None, :] == wanted[:, None]).astype(jnp.int32)
        return jnp.sum(hit * values[None, :], axis=1)

    return (send_slot, pick(send_slot, slots, items), pick(target, items, recv_slot),
            pick(recv_slot, slots, target))


def local(nboson, nblock, gamma_ph, full_ph, chi_ph, pp_vertex, chi_pp, relabel):
    points, rows, order = gamma_ph.shape
    row_tiles, col_blocks = relabel.shape[1] // nblock, relabel.shape[2]
    high, wide = rows // row_tiles, order // col_blocks
    total = points * row_tiles * col_blocks
    capacity = -(-total // nboson) + 1
    bf16, f32 = jnp.bfloat16, jnp.float32
    whole = pltpu.VMEM((points, order, order), bf16)
    shard = pltpu.VMEM(gamma_ph.shape, bf16)
    slabs = pltpu.VMEM((nboson, capacity, high, wide), bf16)
    smem = pl.BlockSpec(memory_space=pltpu.SMEM)
    vmem = pl.BlockSpec(memory_space=pltpu.VMEM)
    hbm = pl.BlockSpec(memory_space=pl.ANY)
    return pl.pallas_call(
        functools.partial(kernel, nboson, nblock, row_tiles, col_blocks),
        out_shape=pltpu.VMEM(gamma_ph.shape, bf16), name="window",
        in_specs=[smem] * 4 + [hbm, hbm, vmem, hbm, vmem], out_specs=vmem,
        scratch_shapes=[
            whole, whole, shard, shard, pltpu.VMEM(gamma_ph.shape, f32),
            pltpu.VMEM((total, high, wide), bf16), slabs, slabs, slabs, slabs,
            DMA, DMA((nboson,)), DMA((nboson,)), DMA((nboson,)), DMA((nboson,)),
        ] + gather_scratch(nblock, points) + gather_scratch(nblock, points),
        compiler_params=pltpu.CompilerParams(
            collective_id=0, has_side_effects=True, vmem_limit_bytes=60 * 1024 * 1024),
    )(*tables(relabel, points, row_tiles, nboson, capacity),
      gamma_ph, full_ph, chi_ph, pp_vertex, chi_pp)


def solution(mesh):
    placed = (
        P("boson", "block", None),
        P("boson", "block", None),
        P("boson", None),
        P("boson", "block", None),
        P("boson", None),
        P(),
    )
    return jax.shard_map(
        functools.partial(local, mesh.shape["boson"], mesh.shape["block"]), mesh=mesh,
        in_specs=placed, out_specs=P("boson", "block", None), check_vma=False,
    )
```

```python
import functools
import jax
import jax.numpy as jnp
from jax import lax
from jax.experimental import pallas as pl
from jax.experimental.pallas import tpu as pltpu
from jax.sharding import PartitionSpec as P

MESH = pl.DeviceIdType.MESH
DMA = pltpu.SemaphoreType.DMA
PARTS = 2
LANES = 128


def loop(start, stop, body):
    lax.fori_loop(start, stop, lambda i, carry: (body(i), carry)[1], 0)


class Gather:
    def __init__(self, nblock, shard, whole, sems):
        self.nblock, self.shard, self.whole = nblock, shard, whole
        self.far_s, self.far_r, self.near_s, self.near_r, self.fwd_s, self.fwd_r, self.loc = sems
        self.points, self.rows, order = shard.shape
        self.cols = order // PARTS
        self.chunks = self.points * PARTS
        self.boson = lax.axis_index("boson")
        self.here = lax.axis_index("block")
        self.partner = self.here + 1 - 2 * (self.here % 2)

    def peers(self):
        out = [self.partner]
        for j in range(1, self.nblock // 2):
            out.append((self.here + 2 * j) % self.nblock)
        return out

    def columns(self, g):
        return pl.ds(pl.multiple_of(g % PARTS * self.cols, self.cols), self.cols)

    def source(self, g):
        return self.shard.at[g // PARTS, :, self.columns(g)]

    def place(self, g, owner):
        rows = pl.ds(pl.multiple_of(owner * self.rows, self.rows), self.rows)
        return self.whole.at[g // PARTS, rows, self.columns(g)]

    def far(self, g, j, owner):
        return pltpu.make_async_remote_copy(
            src_ref=self.source(g), dst_ref=self.place(g, owner),
            send_sem=self.far_s.at[j - 1, g], recv_sem=self.far_r.at[j - 1, g],
            device_id=(self.boson, (self.here + 2 * j) % self.nblock), device_id_type=MESH)

    def near(self, g, owner):
        return pltpu.make_async_remote_copy(
            src_ref=self.source(g), dst_ref=self.place(g, owner),
            send_sem=self.near_s.at[g], recv_sem=self.near_r.at[g],
            device_id=(self.boson, self.partner), device_id_type=MESH)

    def forward(self, g, j, owner):
        return pltpu.make_async_remote_copy(
            src_ref=self.place(g, owner), dst_ref=self.place(g, owner),
            send_sem=self.fwd_s.at[j - 1, g], recv_sem=self.fwd_r.at[j - 1, g],
            device_id=(self.boson, self.partner), device_id_type=MESH)

    def own(self):
        rows = pl.ds(pl.multiple_of(self.here * self.rows, self.rows), self.rows)
        return pltpu.make_async_copy(self.shard, self.whole.at[:, rows], self.loc)

    def each_far(self, act):
        for j in range(1, self.nblock // 2):
            act(j)

    def start(self):
        def one(g):
            self.each_far(lambda j: self.far(g, j, self.here).start())
            self.near(g, self.here).start()
        loop(0, self.chunks, one)

    def relay(self, g):
        def one(j):
            owner = (self.here + self.nblock - 2 * j) % self.nblock
            self.far(g, j, owner).wait_recv()
            self.forward(g, j, owner).start()
        self.each_far(one)

    def arrived(self, g):
        self.near(g, self.partner).wait_recv()
        def one(j):
            twin = (self.partner + self.nblock - 2 * j) % self.nblock
            self.forward(g, j, twin).wait_recv()
        self.each_far(one)

    def sent_far(self):
        loop(0, self.chunks,
             lambda g: self.each_far(lambda j: self.far(g, j, self.here).wait_send()))

    def sent_near(self):
        def one(g):
            self.near(g, self.here).wait_send()
            def fwd(j):
                owner = (self.here + self.nblock - 2 * j) % self.nblock
                self.forward(g, j, owner).wait_send()
            self.each_far(fwd)
        loop(0, self.chunks, one)


def gather_scratch(nblock, points):
    far, chunks = max(nblock // 2 - 1, 1), points * PARTS
    return [DMA((far, chunks)), DMA((far, chunks)), DMA((chunks,)), DMA((chunks,)),
            DMA((far, chunks)), DMA((far, chunks)), DMA]


class Exchange:
    def __init__(self, nboson, outgoing, incoming, send, recv):
        self.n, self.outgoing, self.incoming = nboson, outgoing, incoming
        self.send, self.recv = send, recv
        self.boson = lax.axis_index("boson")
        self.block = lax.axis_index("block")

    def peers(self):
        return [(self.boson + s) % self.n for s in range(1, self.n)]

    def shift(self, i):
        return self.n // 2 + (1 - 2 * (i % 2)) * ((i + 1) // 2)

    def copy(self, s, slot):
        dest = (self.boson + s) % self.n
        return pltpu.make_async_remote_copy(
            src_ref=self.outgoing.at[dest], dst_ref=self.incoming.at[slot],
            send_sem=self.send.at[s], recv_sem=self.recv.at[s],
            device_id=(dest, self.block), device_id_type=MESH)

    def pack(self, target, dest, tiles, table):
        capacity = target.shape[1]
        for k in range(capacity):
            target[dest, k] = tiles[table[dest * capacity + k]]

    def pack_and_start(self, tiles, table):
        def pack(i):
            self.pack(self.outgoing, (self.boson + self.shift(i)) % self.n, tiles, table)
        pack(0)
        def one(i):
            pack(i)
            self.copy(self.shift(i - 1), self.boson).start()
        loop(1, self.n - 1, one)
        self.pack(self.incoming, self.boson, tiles, table)
        self.copy(self.shift(self.n - 2), self.boson).start()

    def received(self):
        loop(1, self.n, lambda s: self.copy(s, (self.boson + self.n - s) % self.n).wait_recv())

    def sent(self):
        loop(1, self.n, lambda s: self.copy(s, self.boson).wait_send())


def greet(block_peers, boson_peers):
    barrier = pltpu.get_barrier_semaphore()
    boson, block = lax.axis_index("boson"), lax.axis_index("block")
    for peer in block_peers:
        pl.semaphore_signal(barrier, inc=1, device_id=(boson, peer), device_id_type=MESH)
    for peer in boson_peers:
        pl.semaphore_signal(barrier, inc=1, device_id=(peer, block), device_id_type=MESH)
    pl.semaphore_wait(barrier, len(block_peers) + len(boson_peers))


def slot_tables(nboson, capacity, targets, rows):
    row_tiles, col_blocks, _ = targets.shape
    per_point = row_tiles * col_blocks
    points = targets.shape[2] // nboson
    total = points * per_point
    boson = lax.axis_index("boson")
    flat = targets[...].reshape(per_point, targets.shape[2])
    lane = lax.broadcasted_iota(jnp.int32, flat.shape, 1)
    own = jnp.concatenate(
        [jnp.sum(jnp.where(lane == boson * points + q, flat, 0), axis=1, keepdims=True)
         for q in range(points)], axis=0)
    item = lax.broadcasted_iota(jnp.int32, (total, 1), 0)

    def spread(keys, values, width):
        wanted = lax.broadcasted_iota(jnp.int32, (total, width), 1)
        return jnp.sum(jnp.where(keys == wanted, values, 0), axis=0, keepdims=True)

    shift = ((own >> (points.bit_length() - 1)) - boson) & (nboson - 1)
    target = (own & (points - 1)) * per_point + (item & (per_point - 1))
    other = lax.broadcasted_iota(jnp.int32, (total, total), 1)
    earlier = (spread(item, shift, total) == shift) & (other < item)
    rank = jnp.sum(jnp.where(earlier, 1, 0), axis=1, keepdims=True)
    send = ((boson + shift) & (nboson - 1)) * capacity + rank
    recv = ((boson - shift) & (nboson - 1)) * capacity + rank
    width = rows.shape[0] // 8 * rows.shape[1]
    last_slot, last_item = nboson * capacity - 1, total - 1
    for k, (keys, values, last) in enumerate((
            (item, send, last_slot), (send, item, last_item),
            (target, recv, last_slot), (recv, target, last_item))):
        line = jnp.minimum(spread(keys, values, width), last)
        for h in range(width // LANES):
            rows[h * 8 + k:h * 8 + k + 1, :] = line[:, h * LANES:(h + 1) * LANES]


class Table:
    def __init__(self, ref, k):
        self.ref, self.k = ref, k

    def __getitem__(self, i):
        return self.ref[i // LANES * 8 + self.k, i % LANES]


def kernel(nboson, nblock, row_tiles, col_blocks,
           relabel, gamma_in, full_in, chi_ph, pp_in, chi_pp, out,
           full, pp, gamma, scaled, base, tiles, packed, landed, back, returned,
           targets, table_rows, table,
           gamma_sem, table_sem, ahead_s, ahead_r, home_s, home_r, *gather_sems):
    half = len(gather_sems) // 2
    first = Gather(nblock, full_in, full, gather_sems[:half])
    second = Gather(nblock, pp_in, pp, gather_sems[half:])
    ahead = Exchange(nboson, packed, landed, ahead_s, ahead_r)
    home = Exchange(nboson, back, returned, home_s, home_r)
    points, rows, order = gamma.shape
    high, wide = rows // row_tiles, order // col_blocks
    step = 2 * wide
    capacity = landed.shape[1]
    send_slot, item_of, back_slot, back_item_of = (Table(table, i) for i in range(4))
    block_rows = pl.ds(lax.axis_index("block") * row_tiles, row_tiles)
    load_targets = pltpu.make_async_copy(relabel.at[block_rows], targets, table_sem.at[0])
    load_table = pltpu.make_async_copy(table_rows, table, table_sem.at[1])
    load_gamma = pltpu.make_async_copy(gamma_in, gamma, gamma_sem)

    first.own().start()
    load_gamma.start()
    load_targets.start()
    second.own().start()
    greet(first.peers(), ahead.peers())
    first.start()

    load_gamma.wait()
    for q in range(points):
        scaled[q] = (gamma[q].astype(jnp.float32) * chi_ph[q:q + 1, :]).astype(jnp.bfloat16)
    load_targets.wait()
    slot_tables(nboson, capacity, targets, table_rows)
    load_table.start()
    first.own().wait()

    def cut(wire, q, column):
        for r in range(row_tiles):
            for k in range(2):
                item = (q * row_tiles + r) * col_blocks + column * 2 + k
                tiles[item] = wire[r * high:(r + 1) * high, k * wide:(k + 1) * wide]

    def product(whole, q, column):
        at = pl.ds(pl.multiple_of(column * step, step), step)
        return at, jnp.dot(scaled[q], whole[q, :, at], preferred_element_type=jnp.float32)

    per_part = order // step // PARTS

    def compute(g):
        first.arrived(g)
        q = g // PARTS
        for n in range(per_part):
            column = g % PARTS * per_part + n
            at, phi = product(full, q, column)
            base[q, :, at] = gamma[q, :, at].astype(jnp.float32) + phi
            cut(phi.astype(jnp.bfloat16), q, column)

    first.relay(0)
    def one(g):
        first.relay(g)
        compute(g - 1)
    loop(1, first.chunks, one)
    first.sent_far()
    second.start()
    load_table.wait()
    compute(first.chunks - 1)
    ahead.pack_and_start(tiles, item_of)

    loop(0, second.chunks, second.relay)
    first.sent_near()
    second.own().wait()
    loop(0, second.chunks, second.arrived)
    ahead.received()

    flat = landed.reshape(nboson * capacity, high, wide)
    for p in range(points):
        for c in range(col_blocks):
            chi = chi_pp[p:p + 1, c * wide:(c + 1) * wide]
            for r in range(row_tiles):
                tile = flat[back_slot[(p * row_tiles + r) * col_blocks + c]]
                scaled[p, r * high:(r + 1) * high, c * wide:(c + 1) * wide] = (
                    tile.astype(jnp.float32) * chi).astype(jnp.bfloat16)
    def point(p):
        for column in range(order // step):
            _, phi = product(pp, p, column)
            cut(phi.astype(jnp.bfloat16), p, column)
    loop(0, points, point)
    home.pack_and_start(tiles, back_item_of)
    ahead.sent()
    second.sent_far()
    second.sent_near()
    home.received()

    flat_back = returned.reshape(nboson * capacity, high, wide)
    def finish(q):
        for r in range(row_tiles):
            for c in range(col_blocks):
                tile = flat_back[send_slot[(q * row_tiles + r) * col_blocks + c]]
                at = (q, slice(r * high, (r + 1) * high), slice(c * wide, (c + 1) * wide))
                out[at] = (base[at] + tile.astype(jnp.float32)).astype(jnp.bfloat16)
    loop(0, points, finish)
    home.sent()


def local(nboson, nblock, gamma_ph, full_ph, chi_ph, pp_vertex, chi_pp, relabel):
    points, rows, order = gamma_ph.shape
    row_tiles, col_blocks = relabel.shape[1] // nblock, relabel.shape[2]
    high, wide = rows // row_tiles, order // col_blocks
    total = points * row_tiles * col_blocks
    capacity = -(-total // nboson) + 1
    bf16, f32 = jnp.bfloat16, jnp.float32
    whole = pltpu.VMEM((points, order, order), bf16)
    shard = pltpu.VMEM(gamma_ph.shape, bf16)
    slabs = pltpu.VMEM((nboson, capacity, high, wide), bf16)
    table_rows = -(-(nboson * capacity) // LANES) * 8
    for count in (nboson, points, row_tiles * col_blocks):
        assert count & (count - 1) == 0
    vmem = pl.BlockSpec(memory_space=pltpu.VMEM)
    hbm = pl.BlockSpec(memory_space=pl.ANY)
    return pl.pallas_call(
        functools.partial(kernel, nboson, nblock, row_tiles, col_blocks),
        out_shape=pltpu.VMEM(gamma_ph.shape, bf16), name="window",
        in_specs=[hbm, hbm, hbm, vmem, hbm, vmem], out_specs=vmem,
        scratch_shapes=[
            whole, whole, shard, shard, pltpu.VMEM(gamma_ph.shape, f32),
            pltpu.VMEM((total, high, wide), bf16), slabs, slabs, slabs, slabs,
            pltpu.VMEM((row_tiles,) + (relabel.shape[2], relabel.shape[0]), jnp.int32),
            pltpu.VMEM((table_rows, LANES), jnp.int32), pltpu.SMEM((table_rows, LANES), jnp.int32),
            DMA, DMA((2,)), DMA((nboson,)), DMA((nboson,)), DMA((nboson,)), DMA((nboson,)),
        ] + gather_scratch(nblock, points) + gather_scratch(nblock, points),
        compiler_params=pltpu.CompilerParams(
            collective_id=0, has_side_effects=True, vmem_limit_bytes=60 * 1024 * 1024),
    )(relabel.transpose(1, 2, 0), gamma_ph, full_ph, chi_ph, pp_vertex, chi_pp)


def solution(mesh):
    placed = (
        P("boson", "block", None),
        P("boson", "block", None),
        P("boson", None),
        P("boson", "block", None),
        P("boson", None),
        P(),
    )
    return jax.shard_map(
        functools.partial(local, mesh.shape["boson"], mesh.shape["block"]), mesh=mesh,
        in_specs=placed, out_specs=P("boson", "block", None), check_vma=False,
    )
```

```python
import functools
import jax
import jax.numpy as jnp
from jax import lax
from jax.experimental import pallas as pl
from jax.experimental.pallas import tpu as pltpu
from jax.sharding import PartitionSpec as P

MESH = pl.DeviceIdType.MESH
DMA = pltpu.SemaphoreType.DMA
PARTS = 2
LANES = 128


def loop(start, stop, body):
    lax.fori_loop(start, stop, lambda i, carry: (body(i), carry)[1], 0)


class Gather:
    def __init__(self, nblock, shard, whole, sems):
        self.nblock, self.shard, self.whole = nblock, shard, whole
        self.far_s, self.far_r, self.near_s, self.near_r, self.fwd_s, self.fwd_r, self.loc = sems
        self.points, self.rows, order = shard.shape
        self.cols = order // PARTS
        self.chunks = self.points * PARTS
        self.boson = lax.axis_index("boson")
        self.here = lax.axis_index("block")
        self.partner = self.here + 1 - 2 * (self.here % 2)

    def peers(self):
        out = [self.partner]
        for j in range(1, self.nblock // 2):
            out.append((self.here + 2 * j) % self.nblock)
        return out

    def columns(self, g):
        return pl.ds(pl.multiple_of(g % PARTS * self.cols, self.cols), self.cols)

    def source(self, g):
        return self.shard.at[g // PARTS, :, self.columns(g)]

    def place(self, g, owner):
        rows = pl.ds(pl.multiple_of(owner * self.rows, self.rows), self.rows)
        return self.whole.at[g // PARTS, rows, self.columns(g)]

    def far(self, g, j, owner):
        return pltpu.make_async_remote_copy(
            src_ref=self.source(g), dst_ref=self.place(g, owner),
            send_sem=self.far_s.at[j - 1, g], recv_sem=self.far_r.at[j - 1, g],
            device_id=(self.boson, (self.here + 2 * j) % self.nblock), device_id_type=MESH)

    def near(self, g, owner):
        return pltpu.make_async_remote_copy(
            src_ref=self.source(g), dst_ref=self.place(g, owner),
            send_sem=self.near_s.at[g], recv_sem=self.near_r.at[g],
            device_id=(self.boson, self.partner), device_id_type=MESH)

    def forward(self, g, j, owner):
        return pltpu.make_async_remote_copy(
            src_ref=self.place(g, owner), dst_ref=self.place(g, owner),
            send_sem=self.fwd_s.at[j - 1, g], recv_sem=self.fwd_r.at[j - 1, g],
            device_id=(self.boson, self.partner), device_id_type=MESH)

    def own(self):
        rows = pl.ds(pl.multiple_of(self.here * self.rows, self.rows), self.rows)
        return pltpu.make_async_copy(self.shard, self.whole.at[:, rows], self.loc)

    def each_far(self, act):
        for j in range(1, self.nblock // 2):
            act(j)

    def start(self):
        def one(g):
            self.each_far(lambda j: self.far(g, j, self.here).start())
            self.near(g, self.here).start()
        loop(0, self.chunks, one)

    def relay(self, g):
        def one(j):
            owner = (self.here + self.nblock - 2 * j) % self.nblock
            self.far(g, j, owner).wait_recv()
            self.forward(g, j, owner).start()
        self.each_far(one)

    def arrived(self, g):
        self.near(g, self.partner).wait_recv()
        def one(j):
            twin = (self.partner + self.nblock - 2 * j) % self.nblock
            self.forward(g, j, twin).wait_recv()
        self.each_far(one)

    def sent_far(self):
        loop(0, self.chunks,
             lambda g: self.each_far(lambda j: self.far(g, j, self.here).wait_send()))

    def sent_near(self):
        def one(g):
            self.near(g, self.here).wait_send()
            def fwd(j):
                owner = (self.here + self.nblock - 2 * j) % self.nblock
                self.forward(g, j, owner).wait_send()
            self.each_far(fwd)
        loop(0, self.chunks, one)


def gather_scratch(nblock, points):
    far, chunks = max(nblock // 2 - 1, 1), points * PARTS
    return [DMA((far, chunks)), DMA((far, chunks)), DMA((chunks,)), DMA((chunks,)),
            DMA((far, chunks)), DMA((far, chunks)), DMA]


class Exchange:
    def __init__(self, nboson, outgoing, incoming, send, recv):
        self.n, self.outgoing, self.incoming = nboson, outgoing, incoming
        self.send, self.recv = send, recv
        self.boson = lax.axis_index("boson")
        self.block = lax.axis_index("block")

    def peers(self):
        return [(self.boson + s) % self.n for s in range(1, self.n)]

    def shift(self, i):
        upper = self.boson // (self.n // 2)
        return (i + 1) * (1 - upper) + (self.n - 1 - i) * upper

    def copy(self, s, slot):
        dest = (self.boson + s) % self.n
        return pltpu.make_async_remote_copy(
            src_ref=self.outgoing.at[dest], dst_ref=self.incoming.at[slot],
            send_sem=self.send.at[s], recv_sem=self.recv.at[s],
            device_id=(dest, self.block), device_id_type=MESH)

    def pack(self, target, dest, tiles, table):
        capacity = target.shape[1]
        for k in range(capacity):
            target[dest, k] = tiles[table[dest * capacity + k]]

    def pack_and_start(self, tiles, table):
        def pack(i):
            self.pack(self.outgoing, (self.boson + self.shift(i)) % self.n, tiles, table)
        pack(0)
        def one(i):
            pack(i)
            self.copy(self.shift(i - 1), self.boson).start()
        loop(1, self.n - 1, one)
        self.pack(self.incoming, self.boson, tiles, table)
        self.copy(self.shift(self.n - 2), self.boson).start()

    def received(self):
        loop(1, self.n, lambda s: self.copy(s, (self.boson + self.n - s) % self.n).wait_recv())

    def sent(self):
        loop(1, self.n, lambda s: self.copy(s, self.boson).wait_send())


def greet(block_peers, boson_peers):
    barrier = pltpu.get_barrier_semaphore()
    boson, block = lax.axis_index("boson"), lax.axis_index("block")
    for peer in block_peers:
        pl.semaphore_signal(barrier, inc=1, device_id=(boson, peer), device_id_type=MESH)
    for peer in boson_peers:
        pl.semaphore_signal(barrier, inc=1, device_id=(peer, block), device_id_type=MESH)
    pl.semaphore_wait(barrier, len(block_peers) + len(boson_peers))


def slot_tables(nboson, capacity, targets, rows):
    row_tiles, col_blocks, _ = targets.shape
    per_point = row_tiles * col_blocks
    points = targets.shape[2] // nboson
    total = points * per_point
    boson = lax.axis_index("boson")
    flat = targets[...].reshape(per_point, targets.shape[2])
    lane = lax.broadcasted_iota(jnp.int32, flat.shape, 1)
    own = jnp.concatenate(
        [jnp.sum(jnp.where(lane == boson * points + q, flat, 0), axis=1, keepdims=True)
         for q in range(points)], axis=0)
    item = lax.broadcasted_iota(jnp.int32, (total, 1), 0)

    def spread(keys, values, width):
        wanted = lax.broadcasted_iota(jnp.int32, (total, width), 1)
        return jnp.sum(jnp.where(keys == wanted, values, 0), axis=0, keepdims=True)

    shift = ((own >> (points.bit_length() - 1)) - boson) & (nboson - 1)
    target = (own & (points - 1)) * per_point + (item & (per_point - 1))
    other = lax.broadcasted_iota(jnp.int32, (total, total), 1)
    earlier = (spread(item, shift, total) == shift) & (other < item)
    rank = jnp.sum(jnp.where(earlier, 1, 0), axis=1, keepdims=True)
    send = ((boson + shift) & (nboson - 1)) * capacity + rank
    recv = ((boson - shift) & (nboson - 1)) * capacity + rank
    width = rows.shape[0] // 8 * rows.shape[1]
    last_slot, last_item = nboson * capacity - 1, total - 1
    for k, (keys, values, last) in enumerate((
            (item, send, last_slot), (send, item, last_item),
            (target, recv, last_slot), (recv, target, last_item))):
        line = jnp.minimum(spread(keys, values, width), last)
        for h in range(width // LANES):
            rows[h * 8 + k:h * 8 + k + 1, :] = line[:, h * LANES:(h + 1) * LANES]


class Table:
    def __init__(self, ref, k):
        self.ref, self.k = ref, k

    def __getitem__(self, i):
        return self.ref[i // LANES * 8 + self.k, i % LANES]


def kernel(nboson, nblock, row_tiles, col_blocks,
           relabel, gamma_in, full_in, chi_ph, pp_in, chi_pp, out,
           full, pp, gamma, scaled, base, tiles, packed, landed, back, returned,
           targets, table_rows, table,
           gamma_sem, table_sem, ahead_s, ahead_r, home_s, home_r, *gather_sems):
    half = len(gather_sems) // 2
    first = Gather(nblock, full_in, full, gather_sems[:half])
    second = Gather(nblock, pp_in, pp, gather_sems[half:])
    ahead = Exchange(nboson, packed, landed, ahead_s, ahead_r)
    home = Exchange(nboson, back, returned, home_s, home_r)
    points, rows, order = gamma.shape
    high, wide = rows // row_tiles, order // col_blocks
    step = 2 * wide
    capacity = landed.shape[1]
    send_slot, item_of, back_slot, back_item_of = (Table(table, i) for i in range(4))
    block_rows = pl.ds(lax.axis_index("block") * row_tiles, row_tiles)
    load_targets = pltpu.make_async_copy(relabel.at[block_rows], targets, table_sem.at[0])
    load_table = pltpu.make_async_copy(table_rows, table, table_sem.at[1])
    load_gamma = pltpu.make_async_copy(gamma_in, gamma, gamma_sem)

    first.own().start()
    load_gamma.start()
    load_targets.start()
    second.own().start()
    greet(first.peers(), ahead.peers())
    first.start()

    load_gamma.wait()
    for q in range(points):
        scaled[q] = (gamma[q].astype(jnp.float32) * chi_ph[q:q + 1, :]).astype(jnp.bfloat16)
    load_targets.wait()
    slot_tables(nboson, capacity, targets, table_rows)
    load_table.start()
    first.own().wait()

    def cut(wire, q, column):
        for r in range(row_tiles):
            for k in range(2):
                item = (q * row_tiles + r) * col_blocks + column * 2 + k
                tiles[item] = wire[r * high:(r + 1) * high, k * wide:(k + 1) * wide]

    def product(whole, q, column):
        at = pl.ds(pl.multiple_of(column * step, step), step)
        return at, jnp.dot(scaled[q], whole[q, :, at], preferred_element_type=jnp.float32)

    per_part = order // step // PARTS

    def compute(g):
        first.arrived(g)
        q = g // PARTS
        for n in range(per_part):
            column = g % PARTS * per_part + n
            at, phi = product(full, q, column)
            base[q, :, at] = gamma[q, :, at].astype(jnp.float32) + phi
            cut(phi.astype(jnp.bfloat16), q, column)

    first.relay(0)
    def one(g):
        first.relay(g)
        compute(g - 1)
    loop(1, first.chunks, one)
    first.sent_far()
    second.start()
    load_table.wait()
    compute(first.chunks - 1)
    ahead.pack_and_start(tiles, item_of)

    loop(0, second.chunks, second.relay)
    first.sent_near()
    second.own().wait()
    loop(0, second.chunks, second.arrived)
    ahead.received()

    flat = landed.reshape(nboson * capacity, high, wide)
    for p in range(points):
        for c in range(col_blocks):
            chi = chi_pp[p:p + 1, c * wide:(c + 1) * wide]
            for r in range(row_tiles):
                tile = flat[back_slot[(p * row_tiles + r) * col_blocks + c]]
                scaled[p, r * high:(r + 1) * high, c * wide:(c + 1) * wide] = (
                    tile.astype(jnp.float32) * chi).astype(jnp.bfloat16)
    def point(p):
        for column in range(order // step):
            _, phi = product(pp, p, column)
            cut(phi.astype(jnp.bfloat16), p, column)
    loop(0, points, point)
    home.pack_and_start(tiles, back_item_of)
    ahead.sent()
    second.sent_far()
    second.sent_near()
    home.received()

    flat_back = returned.reshape(nboson * capacity, high, wide)
    def finish(q):
        for r in range(row_tiles):
            for c in range(col_blocks):
                tile = flat_back[send_slot[(q * row_tiles + r) * col_blocks + c]]
                at = (q, slice(r * high, (r + 1) * high), slice(c * wide, (c + 1) * wide))
                out[at] = (base[at] + tile.astype(jnp.float32)).astype(jnp.bfloat16)
    loop(0, points, finish)
    home.sent()


def local(nboson, nblock, gamma_ph, full_ph, chi_ph, pp_vertex, chi_pp, relabel):
    points, rows, order = gamma_ph.shape
    row_tiles, col_blocks = relabel.shape[1] // nblock, relabel.shape[2]
    high, wide = rows // row_tiles, order // col_blocks
    total = points * row_tiles * col_blocks
    capacity = -(-total // nboson) + 1
    bf16, f32 = jnp.bfloat16, jnp.float32
    whole = pltpu.VMEM((points, order, order), bf16)
    shard = pltpu.VMEM(gamma_ph.shape, bf16)
    slabs = pltpu.VMEM((nboson, capacity, high, wide), bf16)
    table_rows = -(-(nboson * capacity) // LANES) * 8
    for count in (nboson, points, row_tiles * col_blocks):
        assert count & (count - 1) == 0
    vmem = pl.BlockSpec(memory_space=pltpu.VMEM)
    hbm = pl.BlockSpec(memory_space=pl.ANY)
    return pl.pallas_call(
        functools.partial(kernel, nboson, nblock, row_tiles, col_blocks),
        out_shape=pltpu.VMEM(gamma_ph.shape, bf16), name="window",
        in_specs=[hbm, hbm, hbm, vmem, hbm, vmem], out_specs=vmem,
        scratch_shapes=[
            whole, whole, shard, shard, pltpu.VMEM(gamma_ph.shape, f32),
            pltpu.VMEM((total, high, wide), bf16), slabs, slabs, slabs, slabs,
            pltpu.VMEM((row_tiles,) + (relabel.shape[2], relabel.shape[0]), jnp.int32),
            pltpu.VMEM((table_rows, LANES), jnp.int32), pltpu.SMEM((table_rows, LANES), jnp.int32),
            DMA, DMA((2,)), DMA((nboson,)), DMA((nboson,)), DMA((nboson,)), DMA((nboson,)),
        ] + gather_scratch(nblock, points) + gather_scratch(nblock, points),
        compiler_params=pltpu.CompilerParams(
            collective_id=0, has_side_effects=True, vmem_limit_bytes=60 * 1024 * 1024),
    )(relabel.transpose(1, 2, 0), gamma_ph, full_ph, chi_ph, pp_vertex, chi_pp)


def solution(mesh):
    placed = (
        P("boson", "block", None),
        P("boson", "block", None),
        P("boson", None),
        P("boson", "block", None),
        P("boson", None),
        P(),
    )
    return jax.shard_map(
        functools.partial(local, mesh.shape["boson"], mesh.shape["block"]), mesh=mesh,
        in_specs=placed, out_specs=P("boson", "block", None), check_vma=False,
    )
```
